256 devices in a mesh: grp: 4 (over x_lo, core), shard: 64 (over z, y, x_hi).
Axes of the slice: x: 4 (x_hi: 2, x_lo: 2; x = x_hi * 2 + x_lo), y: 4, z: 8, core: 2. Of those that a mesh axis runs over, the one named last changes fastest.
Arguments:
- tokens: bfloat16 [8192, 1280], P('shard'), may hold values from -6 to 6
- fc1_mean: float32 [5120, 1280], P('shard'), may hold values from -0.15625 to 0.15625
- fc1_variance: float32 [5120, 1280], P('shard'), may hold values from 1e-05 to 0.001
- fc1_deviation: bfloat16 [20, 5120, 1280], P(None, 'shard'), may hold values from -0.19921875 to 0.19921875
- fc2_mean: float32 [1280, 5120], P(None, 'shard'), may hold values from -0.078125 to 0.078125
- fc2_variance: float32 [1280, 5120], P(None, 'shard'), may hold values from 2.5e-06 to 0.00025
- fc2_deviation: bfloat16 [20, 1280, 5120], P(None, None, 'shard'), may hold values from -0.099609375 to 0.099609375
- noise_fc1: bfloat16 [8, 5120, 1280], P('grp', 'shard'), may hold values from -6 to 6
- noise_fc2: bfloat16 [8, 1280, 5120], P('grp', None, 'shard'), may hold values from -6 to 6
- noise_low: float32 [8, 20], P('grp'), may hold values from -4 to 4
Outputs:
- prediction: bfloat16 [8192, 1280], P('shard', 'grp')
The draws below stay inside these ranges and needn't reach their ends.
All inputs are finite; a program needn't handle non-finite values.
Results may differ from the reference program's by a relative error of at most 0.013.
Values may be sent and summed in bfloat16 or wider, within the bound.
No kernel may reach another device: no remote copies, remote signals or barrier semaphores. Data moves between devices by JAX's collectives and lax.ppermute only.
A program may use at most 128 MiB of HBM per device.

```python
import math
import jax
import jax.numpy as jnp
from jax import lax

D = 1280
FF = 5120
K = 20
SAMPLES = 8
TOKENS = 8192


def block_levels(own_key, dims, cuts, least, largest):
    gain, own = 1.0, jax.random.fold_in(own_key, 6)
    for axis_at, parts in cuts:
        steps = jnp.exp(jax.random.uniform(jax.random.fold_in(own, axis_at), (parts,), jnp.float32, least / len(cuts), largest / len(cuts)))
        gain = gain * jnp.repeat(steps, dims[axis_at] // parts).reshape([-1 if axis == axis_at else 1 for axis in range(len(dims))])
    return gain


def bell_draw(own_key, dims, scale, most, split=(), kind=jnp.bfloat16):
    values = scale * jax.random.normal(own_key, dims, jnp.float32)
    if split:
        values = values * block_levels(own_key, dims, split, -0.22, 0.18)
    return jnp.clip(values, -most, most).astype(kind)


def setup_inputs(seed: int = 0) -> dict:
    arg_keys = jax.random.split(jax.random.key(seed), 11)
    return {
        "tokens": bell_draw(arg_keys[0], (TOKENS, D), 1.0, 6.0, ((0, 64),)),
        "fc1_mean": bell_draw(arg_keys[1], (FF, D), D ** -0.5, 0.15625, ((0, 64),), jnp.float32),
        "fc1_variance": jnp.clip(jnp.exp(math.log(0.001) - 4.6051703 * jax.random.uniform(arg_keys[2], (FF, D), jnp.float32) ** block_levels(arg_keys[2], (FF, D), ((0, 64),), -0.2, 0.2)), 9.999999747378752e-06, 0.001),
        "fc1_deviation": bell_draw(arg_keys[3], (K, FF, D), 0.03, 0.19921875, ((1, 64),)),
        "fc2_mean": bell_draw(arg_keys[4], (D, FF), FF ** -0.5, 0.078125, ((1, 64),), jnp.float32),
        "fc2_variance": jnp.clip(jnp.exp(math.log(0.00025) - 4.6051703 * jax.random.uniform(arg_keys[5], (D, FF), jnp.float32) ** block_levels(arg_keys[5], (D, FF), ((1, 64),), -0.2, 0.2)), 2.499999936844688e-06, 0.00025),
        "fc2_deviation": bell_draw(arg_keys[6], (K, D, FF), 0.015, 0.099609375, ((2, 64),)),
        "noise_fc1": bell_draw(arg_keys[7], (SAMPLES, FF, D), 1.0, 6.0, ((0, 4), (1, 64))),
        "noise_fc2": bell_draw(arg_keys[8], (SAMPLES, D, FF), 1.0, 6.0, ((0, 4), (2, 64))),
        "noise_low": bell_draw(arg_keys[9], (SAMPLES, K), 1.0, 4.0, ((0, 4),), jnp.float32),
    }


def sample_weights(moment_mean, moment_variance, deviation, noise_diag, low_half):
    columns = deviation.shape[0]
    flattened = deviation.reshape(columns, -1)
    low_rank = jnp.dot(low_half, flattened, preferred_element_type=jnp.float32)
    low_rank = low_rank.reshape((low_half.shape[0],) + moment_mean.shape)
    sampled = moment_mean[None] + jnp.sqrt(moment_variance)[None] * noise_diag.astype(jnp.float32)
    sampled = sampled + low_rank / math.sqrt(2.0 * (columns - 1))
    return sampled.astype(jnp.bfloat16)

def reference(tokens, fc1_mean, fc1_variance, fc1_deviation, fc2_mean, fc2_variance, fc2_deviation, noise_fc1, noise_fc2, noise_low):
    low_half = noise_low.astype(jnp.bfloat16)
    up_weights = sample_weights(fc1_mean, fc1_variance, fc1_deviation, noise_fc1, low_half)
    down_weights = sample_weights(fc2_mean, fc2_variance, fc2_deviation, noise_fc2, low_half)

    def accumulate(running, weight_pair):
        first_w, second_w = weight_pair
        preact = jnp.dot(tokens, first_w.T, preferred_element_type=jnp.float32)
        hidden = jax.nn.gelu(preact, approximate=False).astype(jnp.bfloat16)
        return (running + jnp.dot(hidden, second_w.T, preferred_element_type=jnp.float32), None)
    start_sum = jnp.zeros((tokens.shape[0], tokens.shape[1]), jnp.float32)
    summed, _ = lax.scan(accumulate, start_sum, (up_weights, down_weights))
    return (summed / SAMPLES).astype(jnp.bfloat16)
```

```python
import math

import jax
import jax.numpy as jnp
from jax import lax
from jax.experimental import pallas as pl
from jax.experimental.pallas import tpu as pltpu
from jax.sharding import Mesh
from jax.sharding import PartitionSpec as P


XL, CORE, Z, Y, XH = "xl", "core", "z", "y", "xh"
SQRT_HALF = math.sqrt(0.5)


def shifted(value, axis, step):
    count = lax.axis_size(axis)
    return lax.ppermute(value, axis, [(i, (i + step) % count) for i in range(count)])


def swapped(value, axes):
    count = 2 ** len(axes)
    name = axes if len(axes) > 1 else axes[0]
    return lax.ppermute(value, name, [(i, i ^ (count - 1)) for i in range(count)])


def sample_kernel(low_ref, mean_ref, var_ref, dev_ref, noise_ref, out_ref):
    columns, _, width = dev_ref.shape
    samples = noise_ref.shape[0]
    part = width // 2
    for at in range(0, width, part):
        cols = slice(at, at + part)
        total = [None] * samples
        for k in range(columns):
            column = dev_ref[k, :, cols].astype(jnp.float32)
            for s in range(samples):
                term = low_ref[s, k] * column
                total[s] = term if k == 0 else total[s] + term
        spread = jnp.sqrt(var_ref[:, cols])
        for s in range(samples):
            noise = noise_ref[s, :, cols].astype(jnp.float32)
            value = mean_ref[:, cols] + spread * noise + total[s]
            out_ref[s, :, cols] = value.astype(jnp.bfloat16)


def sampled_weights(low, mean, var, dev, noise):
    rows, width = mean.shape
    columns, samples = dev.shape[0], noise.shape[0]
    step = 16
    flat = pl.BlockSpec((step, width), lambda i: (i, 0))
    return pl.pallas_call(
        sample_kernel,
        grid=(rows // step,),
        in_specs=[
            pl.BlockSpec(memory_space=pltpu.SMEM),
            flat,
            flat,
            pl.BlockSpec((columns, step, width), lambda i: (0, i, 0)),
            pl.BlockSpec((samples, step, width), lambda i: (0, i, 0)),
        ],
        out_specs=pl.BlockSpec((samples, step, width), lambda i: (0, i, 0)),
        out_shape=jax.ShapeDtypeStruct((samples, rows, width), jnp.bfloat16),
        cost_estimate=pl.CostEstimate(
            flops=4 * columns * rows * width,
            transcendentals=rows * width,
            bytes_accessed=(columns + 8) * rows * width * 2,
        ),
        name="sample",
    )(low, mean, var, dev, noise)


def gelu(x):
    return 0.5 * x * (1.0 + lax.erf(x * SQRT_HALF))


def mlp_kernel(plan, own_count, part_count, place_ref, *refs):
    count = 2 * own_count + 2 * part_count
    ins = refs[:count]
    keep_ref, send_ref, x_buf, up_buf, down_buf, sems = refs[count:]
    xl, core = place_ref[0], place_ref[1]
    copies = []

    def copy_in(src, dst):
        copy = pltpu.make_async_copy(src, dst, sems.at[len(copies)])
        copy.start()
        copies.append(copy)

    half = x_buf.shape[3]
    at = 0
    for buf in (up_buf, down_buf):
        row = 0
        for _ in range(part_count):
            rows = ins[at].shape[0]
            copy_in(ins[at], buf.at[pl.ds(row, rows)])
            row += rows
            at += 1
    for side in range(2):
        for slot, x_half in plan:
            where = jnp.where(core == 1, 1 - side, side)
            target = x_buf.at[slot, where]
            copy_in(ins[at], target if x_half is None else target.at[x_half])
            at += 1
    for copy in copies:
        copy.wait()

    slots = x_buf.shape[0]
    width = x_buf.shape[-1]
    group = min(2, slots)
    wide = lax.broadcasted_iota(jnp.int32, (1, width // 2), 1) < width // 4

    def step(i, carry):
        first = pl.multiple_of(i * group, group)
        x = x_buf[pl.ds(first, group)].reshape(group * 4 * half, width)
        pre = lax.dot_general(
            x, up_buf[...], (((1,), (1,)), ((), ())), preferred_element_type=jnp.float32
        )
        hidden = gelu(pre).astype(jnp.bfloat16)
        out = jnp.dot(hidden, down_buf[...], preferred_element_type=jnp.float32)
        out = out.reshape(group, 2, 2 * half, width)
        for j in range(2):
            cols = slice(j * (width // 2), (j + 1) * (width // 2))
            for g in range(group):
                lower, upper = out[g, 0, :, cols], out[g, 1, :, cols]
                zero = jnp.where(wide, lower, pltpu.roll(upper, width // 4, 1))
                one = jnp.where(wide, pltpu.roll(lower, width // 4, 1), upper)
                zero = zero.astype(jnp.bfloat16)
                one = one.astype(jnp.bfloat16)
                keep = jnp.where(core == 0, zero, one)
                send = jnp.where(core == 0, one, zero)
                way = jnp.where(xl == 1, 1 - j, j)
                for h in range(2):
                    rows = slice(h * half, (h + 1) * half)
                    keep_ref[way, h, first + g] = keep[rows]
                    send_ref[way, h, first + g] = send[rows]
        return carry

    lax.fori_loop(0, slots // group, step, 0)


def mlp(place, slots, plan, own, partner, up_parts, down_parts):
    width = up_parts[0].shape[-1]
    half = own[0].shape[-2]
    hidden = sum(part.shape[0] for part in up_parts)
    rows = slots * 4 * half
    out = jax.ShapeDtypeStruct((2, 2, slots, half, width // 2), jnp.bfloat16)
    ins = [*up_parts, *down_parts, *own, *partner]

    def kernel(*refs):
        mlp_kernel(plan, len(own), len(up_parts), *refs)

    return pl.pallas_call(
        kernel,
        in_specs=[pl.BlockSpec(memory_space=pltpu.SMEM)]
        + [pl.BlockSpec(memory_space=pl.ANY)] * len(ins),
        out_specs=[pl.BlockSpec(memory_space=pltpu.VMEM)] * 2,
        out_shape=[out, out],
        scratch_shapes=[
            pltpu.VMEM((slots, 2, 2, half, width), jnp.bfloat16),
            pltpu.VMEM((hidden, width), jnp.bfloat16),
            pltpu.VMEM((hidden, width), jnp.bfloat16),
            pltpu.SemaphoreType.DMA((len(ins),)),
        ],
        compiler_params=pltpu.CompilerParams(vmem_limit_bytes=48 * 2**20),
        cost_estimate=pl.CostEstimate(
            flops=4 * rows * hidden * width,
            transcendentals=rows * hidden,
            bytes_accessed=rows * width * 4 + hidden * width * 4,
        ),
        name="mlp",
    )(place, *ins)


def ring_gathered(own):
    rows = own.shape[0]
    below = shifted(own, Y, 1)
    above = shifted(own, Y, -1)
    far_low = shifted(below[: rows // 2], Y, 1)
    far_high = shifted(above[rows // 2 :], Y, -1)
    return [own, below, above, far_low, far_high]


def body(
    tokens,
    fc1_mean,
    fc1_variance,
    fc1_deviation,
    fc2_mean,
    fc2_variance,
    fc2_deviation,
    noise_fc1,
    noise_fc2,
    noise_low,
):
    columns = fc1_deviation.shape[0]
    width = tokens.shape[1]
    half = tokens.shape[0] // 2
    xl, core = lax.axis_index(XL), lax.axis_index(CORE)
    place = jnp.stack([xl, core]).astype(jnp.int32)

    mine = lax.dynamic_slice(tokens, (core * half, 0), (half, width))
    across = swapped(mine, (XH,))
    block = jnp.stack([mine, across])

    low = lax.reduce_precision(noise_low, 8, 7) / math.sqrt(2.0 * (columns - 1))
    up = sampled_weights(low, fc1_mean, fc1_variance, fc1_deviation, noise_fc1)
    down = sampled_weights(
        low,
        fc2_mean.T,
        fc2_variance.T,
        jnp.swapaxes(fc2_deviation, 1, 2),
        jnp.swapaxes(noise_fc2, 1, 2),
    )
    up_parts = ring_gathered(up.reshape(-1, width))
    down_parts = ring_gathered(down.reshape(-1, width))

    ring = lax.axis_size(Z)
    blocks, plan = [block], [(0, None)]
    from_below = from_above = block
    for k in range(1, ring // 2):
        from_below = shifted(from_below, Z, 1)
        from_above = shifted(from_above, Z, -1)
        blocks += [from_below, from_above]
        plan += [(ring - k, None), (k, None)]
    blocks += [shifted(from_below[0], Z, 1), shifted(from_above[1], Z, -1)]
    plan += [(ring // 2, 0), (ring // 2, 1)]
    partner = [swapped(b, (CORE,)) for b in blocks]

    keep, send = mlp(place, ring, plan, blocks, partner, up_parts, down_parts)
    got = swapped(send, (CORE,))

    def both(way, x_half, part):
        rows = slice(0, ring // 2) if part == 0 else slice(ring // 2, ring)
        a, b = keep[way, x_half, rows], got[way, x_half, rows]
        return a.astype(jnp.float32) + b.astype(jnp.float32)

    near, far = (XL,), (XL, XH)
    to_near = swapped(both(0, 1, 0).astype(jnp.bfloat16), near)
    to_far = swapped(both(0, 1, 1).astype(jnp.bfloat16), far)
    near_low = swapped(both(1, 0, 0).astype(jnp.bfloat16), near)
    far_high = swapped(both(1, 1, 1).astype(jnp.bfloat16), far)
    far_low = swapped((both(1, 1, 0) + to_near.astype(jnp.float32)).astype(jnp.bfloat16), far)
    near_high = swapped((both(1, 0, 1) + to_far.astype(jnp.float32)).astype(jnp.bfloat16), near)
    lower = both(0, 0, 0) + near_low.astype(jnp.float32) + far_low.astype(jnp.float32)
    upper = both(0, 0, 1) + near_high.astype(jnp.float32) + far_high.astype(jnp.float32)

    def rows_for(k):
        return lower[k] if k < ring // 2 else upper[k - ring // 2]

    total = rows_for(0)
    for k in range(1, ring):
        total = total + shifted(rows_for(k).astype(jnp.bfloat16), Z, k).astype(jnp.float32)
    samples = noise_low.shape[0] * lax.axis_size(XL) * lax.axis_size(CORE)
    total = (total / samples).astype(jnp.bfloat16)
    return jnp.concatenate([total[:, : width // 4], total[:, width // 4 :]], 0)


def solution(mesh):
    fine = Mesh(mesh.devices.reshape(2, 2, 8, 4, 2), (XL, CORE, Z, Y, XH))
    shard, grp = (Z, Y, XH), (XL, CORE)
    placed = (
        P(shard, None),
        P(shard, None),
        P(shard, None),
        P(None, shard, None),
        P(None, shard),
        P(None, shard),
        P(None, None, shard),
        P(grp, shard, None),
        P(grp, None, shard),
        P(grp, None),
    )
    return jax.shard_map(
        body, mesh=fine, in_specs=placed, out_specs=P(shard, grp), check_vma=False
    )
```

```python
import math

import jax
import jax.numpy as jnp
from jax import lax
from jax.experimental import pallas as pl
from jax.experimental.pallas import tpu as pltpu
from jax.sharding import Mesh
from jax.sharding import PartitionSpec as P


XL, CORE, Z, Y, XH = "xl", "core", "z", "y", "xh"
SQRT_HALF = math.sqrt(0.5)
GROUP = 1


def shifted(value, axis, step):
    count = lax.axis_size(axis)
    return lax.ppermute(value, axis, [(i, (i + step) % count) for i in range(count)])


def swapped(value, axes):
    count = 2 ** len(axes)
    name = axes if len(axes) > 1 else axes[0]
    return lax.ppermute(value, name, [(i, i ^ (count - 1)) for i in range(count)])


def sample_kernel(low_ref, mean_ref, var_ref, dev_ref, noise_ref, out_ref):
    columns, height, width = dev_ref.shape
    samples = noise_ref.shape[0]
    tall, part = 8, width // 2
    for top in range(0, height, tall):
        rows = slice(top, top + tall)
        for at in range(0, width, part):
            cols = slice(at, at + part)
            total = [None] * samples
            for k in range(columns):
                column = dev_ref[k, rows, cols].astype(jnp.float32)
                for s in range(samples):
                    term = low_ref[s, k] * column
                    total[s] = term if k == 0 else total[s] + term
            spread = jnp.sqrt(var_ref[rows, cols])
            for s in range(samples):
                noise = noise_ref[s, rows, cols].astype(jnp.float32)
                value = mean_ref[rows, cols] + spread * noise + total[s]
                out_ref[s, rows, cols] = value.astype(jnp.bfloat16)


def sampled_weights(low, mean, var, dev, noise):
    rows, width = mean.shape
    columns, samples = dev.shape[0], noise.shape[0]
    step = 40
    flat = pl.BlockSpec((step, width), lambda i: (i, 0))
    return pl.pallas_call(
        sample_kernel,
        grid=(rows // step,),
        in_specs=[
            pl.BlockSpec(memory_space=pltpu.SMEM),
            flat,
            flat,
            pl.BlockSpec((columns, step, width), lambda i: (0, i, 0)),
            pl.BlockSpec((samples, step, width), lambda i: (0, i, 0)),
        ],
        out_specs=pl.BlockSpec((samples, step, width), lambda i: (0, i, 0)),
        out_shape=jax.ShapeDtypeStruct((samples, rows, width), jnp.bfloat16),
        cost_estimate=pl.CostEstimate(
            flops=4 * columns * rows * width,
            transcendentals=rows * width,
            bytes_accessed=(columns + 8) * rows * width * 2,
        ),
        name="sample",
    )(low, mean, var, dev, noise)


def gelu(x):
    return 0.5 * x * (1.0 + lax.erf(x * SQRT_HALF))


def mlp_kernel(plan, own_count, part_count, place_ref, *refs):
    count = 2 * own_count + 2 * part_count
    ins = refs[:count]
    keep_ref, send_ref, x_buf, up_buf, down_buf, keep_buf, send_buf, sems, out_sems = refs[count:]
    xl, core = place_ref[0], place_ref[1]
    slots, half, width = x_buf.shape[0], x_buf.shape[3], x_buf.shape[-1]
    group = GROUP
    steps = slots // group
    up_copies, down_copies = [], []
    x_copies = [[] for _ in range(steps)]
    for copies, buf, first in ((up_copies, up_buf, 0), (down_copies, down_buf, part_count)):
        row = 0
        for at in range(first, first + part_count):
            rows = ins[at].shape[0]
            dst = buf.at[pl.ds(row, rows)]
            copies.append(pltpu.make_async_copy(ins[at], dst, sems.at[at]))
            row += rows
    at = 2 * part_count
    for side in range(2):
        for slot, x_half in plan:
            dst = x_buf.at[slot, jnp.where(core == 1, 1 - side, side)]
            dst = dst if x_half is None else dst.at[x_half]
            x_copies[slot // group].append(pltpu.make_async_copy(ins[at], dst, sems.at[at]))
            at += 1
    for copies in (up_copies, x_copies[0], down_copies, *x_copies[1:]):
        for copy in copies:
            copy.start()
    for copy in up_copies:
        copy.wait()

    wide = lax.broadcasted_iota(jnp.int32, (1, width // 2), 1) < width // 4

    def outgoing(i):
        cut = pl.ds(i * group, group)
        return [
            pltpu.make_async_copy(buf.at[:, :, cut], ref.at[:, :, cut], out_sems.at[k, i])
            for k, (buf, ref) in enumerate(((keep_buf, keep_ref), (send_buf, send_ref)))
        ]

    def step(i, carry):
        for k in range(steps):

            @pl.when(i == k)
            def _():
                for copy in x_copies[k]:
                    copy.wait()

        first = pl.multiple_of(i * group, group)
        x = x_buf[pl.ds(first, group)].reshape(group * 4 * half, width)
        pre = lax.dot_general(
            x, up_buf[...], (((1,), (1,)), ((), ())), preferred_element_type=jnp.float32
        )
        hidden = gelu(pre).astype(jnp.bfloat16)

        @pl.when(i == 0)
        def _():
            for copy in down_copies:
                copy.wait()

        out = jnp.dot(hidden, down_buf[...], preferred_element_type=jnp.float32)
        out = out.reshape(group, 2, 2 * half, width)
        for j in range(2):
            cols = slice(j * (width // 2), (j + 1) * (width // 2))
            for g in range(group):
                lower, upper = out[g, 0, :, cols], out[g, 1, :, cols]
                zero = jnp.where(wide, lower, pltpu.roll(upper, width // 4, 1))
                one = jnp.where(wide, pltpu.roll(lower, width // 4, 1), upper)
                zero = zero.astype(jnp.bfloat16)
                one = one.astype(jnp.bfloat16)
                keep = jnp.where(core == 0, zero, one)
                send = jnp.where(core == 0, one, zero)
                way = jnp.where(xl == 1, 1 - j, j)
                for h in range(2):
                    rows = slice(h * half, (h + 1) * half)
                    keep_buf[way, h, first + g] = keep[rows]
                    send_buf[way, h, first + g] = send[rows]
        for copy in outgoing(i):
            copy.start()
        return carry

    lax.fori_loop(0, steps, step, 0)
    for i in range(steps):
        for copy in outgoing(i):
            copy.wait()


def mlp(place, slots, plan, own, partner, up_parts, down_parts):
    width = up_parts[0].shape[-1]
    half = own[0].shape[-2]
    hidden = sum(part.shape[0] for part in up_parts)
    rows = slots * 4 * half
    shape = (2, 2, slots, half, width // 2)
    out = jax.ShapeDtypeStruct(shape, jnp.bfloat16)
    ins = [*up_parts, *down_parts, *own, *partner]

    def kernel(*refs):
        mlp_kernel(plan, len(own), len(up_parts), *refs)

    return pl.pallas_call(
        kernel,
        in_specs=[pl.BlockSpec(memory_space=pltpu.SMEM)]
        + [pl.BlockSpec(memory_space=pl.ANY)] * len(ins),
        out_specs=[pl.BlockSpec(memory_space=pl.ANY)] * 2,
        out_shape=[out, out],
        scratch_shapes=[
            pltpu.VMEM((slots, 2, 2, half, width), jnp.bfloat16),
            pltpu.VMEM((hidden, width), jnp.bfloat16),
            pltpu.VMEM((hidden, width), jnp.bfloat16),
            pltpu.VMEM(shape, jnp.bfloat16),
            pltpu.VMEM(shape, jnp.bfloat16),
            pltpu.SemaphoreType.DMA((len(ins),)),
            pltpu.SemaphoreType.DMA((2, slots // GROUP)),
        ],
        compiler_params=pltpu.CompilerParams(vmem_limit_bytes=40 * 2**20),
        cost_estimate=pl.CostEstimate(
            flops=4 * rows * hidden * width,
            transcendentals=rows * hidden,
            bytes_accessed=rows * width * 4 + hidden * width * 4,
        ),
        name="mlp",
    )(place, *ins)


def ring_gathered(own):
    rows = own.shape[0]
    below = shifted(own, Y, 1)
    above = shifted(own, Y, -1)
    far_low = shifted(below[: rows // 2], Y, 1)
    far_high = shifted(above[rows // 2 :], Y, -1)
    return [own, below, above, far_low, far_high]


def summed_over_x(keep, got):
    middle = keep.shape[2] // 2

    def both(way, x_half, rows):
        a, b = keep[way, x_half, rows], got[way, x_half, rows]
        return a.astype(jnp.float32) + b.astype(jnp.float32)

    low, high = slice(0, middle), slice(middle, None)
    near, far = (XL,), (XL, XH)
    to_near = swapped(both(0, 1, low).astype(jnp.bfloat16), near).astype(jnp.float32)
    to_far = swapped(both(0, 1, high).astype(jnp.bfloat16), far).astype(jnp.float32)
    near_sum = jnp.concatenate([both(1, 0, low), both(1, 0, high) + to_far])
    far_sum = jnp.concatenate([both(1, 1, low) + to_near, both(1, 1, high)])
    from_near = swapped(near_sum.astype(jnp.bfloat16), near).astype(jnp.float32)
    from_far = swapped(far_sum.astype(jnp.bfloat16), far).astype(jnp.float32)
    lower = both(0, 0, low) + from_near[low] + from_far[low]
    upper = both(0, 0, high) + from_near[high] + from_far[high]
    return lower, upper


def body(
    tokens,
    fc1_mean,
    fc1_variance,
    fc1_deviation,
    fc2_mean,
    fc2_variance,
    fc2_deviation,
    noise_fc1,
    noise_fc2,
    noise_low,
):
    columns = fc1_deviation.shape[0]
    width = tokens.shape[1]
    half = tokens.shape[0] // 2
    xl, core = lax.axis_index(XL), lax.axis_index(CORE)
    place = jnp.stack([xl, core]).astype(jnp.int32)

    mine = lax.dynamic_slice(tokens, (core * half, 0), (half, width))
    across = swapped(mine, (XH,))
    block = jnp.stack([mine, across])

    low = lax.reduce_precision(noise_low, 8, 7) / math.sqrt(2.0 * (columns - 1))
    up = sampled_weights(low, fc1_mean, fc1_variance, fc1_deviation, noise_fc1)
    down = sampled_weights(
        low,
        fc2_mean.T,
        fc2_variance.T,
        jnp.swapaxes(fc2_deviation, 1, 2),
        jnp.swapaxes(noise_fc2, 1, 2),
    )
    up_parts = ring_gathered(up.reshape(-1, width))
    down_parts = ring_gathered(down.reshape(-1, width))

    ring = lax.axis_size(Z)
    from_below, from_above = shifted(block, Z, 1), shifted(block, Z, -1)
    blocks = {0: [(block, None)], ring - 1: [(from_below, None)], 1: [(from_above, None)]}
    for k in range(2, ring // 2):
        from_below = shifted(from_below, Z, 1)
        from_above = shifted(from_above, Z, -1)
        blocks[ring - k] = [(from_below, None)]
        blocks[k] = [(from_above, None)]
    blocks[ring // 2] = [
        (shifted(from_below[0], Z, 1), 0),
        (shifted(from_above[1], Z, -1), 1),
    ]
    samples = noise_low.shape[0] * lax.axis_size(XL) * lax.axis_size(CORE)
    near_ways = [0, 1, ring - 1, 2]
    far_ways = [k for k in blocks if k not in near_ways]
    summed = {}
    for ways in (near_ways, far_ways):
        own = [entry for k in ways for entry in blocks[k]]
        plan = [(at, x_half) for at, k in enumerate(ways) for _, x_half in blocks[k]]
        own = [value for value, _ in own]
        partner = [swapped(value, (CORE,)) for value in own]
        keep, send = mlp(place, len(ways), plan, own, partner, up_parts, down_parts)
        got = swapped(send, (CORE,))
        lower, upper = summed_over_x(keep, got)
        middle = len(ways) // 2
        for at, k in enumerate(ways):
            summed[k] = lower[at] if at < middle else upper[at - middle]
    total = summed[0]
    for k in near_ways[1:] + far_ways:
        total = total + shifted(summed[k].astype(jnp.bfloat16), Z, k).astype(jnp.float32)
    total = (total / samples).astype(jnp.bfloat16)
    return jnp.concatenate([total[:, : width // 4], total[:, width // 4 :]], 0)


def solution(mesh):
    fine = Mesh(mesh.devices.reshape(2, 2, 8, 4, 2), (XL, CORE, Z, Y, XH))
    shard, grp = (Z, Y, XH), (XL, CORE)
    placed = (
        P(shard, None),
        P(shard, None),
        P(shard, None),
        P(None, shard, None),
        P(None, shard),
        P(None, shard),
        P(None, None, shard),
        P(grp, shard, None),
        P(grp, None, shard),
        P(grp, None),
    )

    return jax.shard_map(
        body, mesh=fine, in_specs=placed, out_specs=P(shard, grp), check_vma=False
    )
```
